128 devices in a mesh: rep: 4 (over y_lo, core), fsdp: 32 (over x, z, y_hi).
Axes of the slice: x: 4, y: 4 (y_hi: 2, y_lo: 2; y = y_hi * 2 + y_lo), z: 4, core: 2. Of those that a mesh axis runs over, the one named last changes fastest.
Arguments:
- acts: bfloat16 [65536, 8192], P(('rep', 'fsdp')), may hold values from -24 to 24
- tok_grads: bfloat16 [65536, 1024], P(('rep', 'fsdp')), may hold values from -64 to 64
- log_ratio: float32 [65536], P(('rep', 'fsdp')), may hold values from -3 to 3
- loss_mask: int32 [65536], P(('rep', 'fsdp')), may hold values 0 or 1
- pairs: int32 [4, 32], P('rep'), may hold values from 0 to 31, each once within a row
- inner_w: float32 [4, 8192, 1024], P('rep', 'fsdp'), may hold values from -6 to 6
- adam_m: float32 [4, 8192, 1024], P('rep', 'fsdp'), may hold values from -3 to 3
- adam_v: float32 [4, 8192, 1024], P('rep', 'fsdp'), may hold values from 0.05 to 1
- anchor: float32 [8192, 1024], P('fsdp'), may hold values from -6 to 6
- outer_mom: float32 [8192, 1024], P('fsdp'), may hold values from -1.75 to 1.75
Outputs:
- input_grad: bfloat16 [65536, 8192], P(('rep', 'fsdp'))
- new_anchor: float32 [8192, 1024], P('fsdp')
- new_mom: float32 [8192, 1024], P('fsdp')
- new_m: float32 [4, 8192, 1024], P('rep', 'fsdp')
The draws below stay inside these ranges and needn't reach their ends.
Inputs may be any that keep to these rules, and one draw needn't show every extreme that they name: Each row of pairs is a permutation of 0 to 31; chosen sequence c of a group pairs with rejected sequence 32 + pairs[r, c].
All inputs are finite; a program needn't handle non-finite values. No bound on the sum of `loss_mask` on one device may be relied on, other than what follows from the above.
Results may differ from the reference program's by a relative error of at most 0.0057.
Values may be sent and summed in bfloat16 or wider, within the bound.
No kernel may reach another device: no remote copies, remote signals or barrier semaphores. Data moves between devices by JAX's collectives and lax.ppermute only.
A program may use at most 128 MiB of HBM per device.

```python
import math
import jax
import jax.numpy as jnp
from jax import lax

D = 8192
KVW = 1024
SEQLEN = 256
SEQ_DEV = 2
HALF = 32
TOKENS = 65536
N_REP = 4
N_FSDP = 32


def plant(drawn, key, smallest, top_value):
    spot = [jax.random.randint(jax.random.fold_in(key, axis), (), 0, length) for axis, length in enumerate(drawn.shape)]
    main_axis = drawn.shape.index(max(drawn.shape))
    beside = spot[:main_axis] + [(spot[main_axis] + 1) % drawn.shape[main_axis]] + spot[main_axis + 1:]
    return drawn.at[tuple(spot)].set(smallest).at[tuple(beside)].set(top_value)


def with_spikes(array, key, source, target, blocks, factor):
    owner, partner = [(jnp.arange(array.shape[dim]) // (array.shape[dim] // blocks)).reshape([-1 if axis == dim else 1 for axis in range(array.ndim)]) for dim in (source, target)]
    chosen = jax.random.permutation(key, blocks)[partner]
    strong = (owner == chosen) | (owner == (partner + blocks // 2) % blocks)
    return jnp.where(strong, factor * array, array)


def block_scale(key, extent, cuts, smallest, top_value):
    gain = 1.0
    for axis_at, blocks in cuts:
        steps = jax.random.uniform(jax.random.fold_in(jax.random.fold_in(key, 6), axis_at), (blocks,), jnp.float32, smallest / len(cuts), top_value / len(cuts))
        gain = gain * jnp.repeat(jnp.exp(steps), extent[axis_at] // blocks).reshape((-1,) + (1,) * (len(extent) - 1 - axis_at))
    return gain


def normal_values(rng, dims, spread, limit, pieces=(), held_as=jnp.bfloat16):
    loudness = block_scale(rng, dims, pieces, -0.22, 0.18) if pieces else 1.0
    drawn = jax.random.normal(rng, dims, jnp.float32) * spread * loudness
    return jnp.minimum(jnp.maximum(drawn, -limit), limit).astype(held_as)


def heavy_noise(own_key, extent, deviation, bound, pieces, heavy, kind=jnp.bfloat16):
    drawn = deviation * jax.random.normal(own_key, extent, jnp.float32)
    if pieces:
        drawn = drawn * block_scale(own_key, extent, pieces, -0.22, 0.18)
    return jnp.clip(with_spikes(drawn, jax.random.fold_in(own_key, 3), *heavy), -bound, bound).astype(kind)


def setup_inputs(seed: int = 0) -> dict:
    splits = jax.random.split(jax.random.key(seed), 11)
    return {
        "acts": heavy_noise(splits[0], (TOKENS, D), 1.0, 24.0, ((0, 128),), (0, 1, 128, 5.5)),
        "tok_grads": normal_values(splits[1], (TOKENS, KVW), 10.0, 64.0, ((0, 128),)),
        "log_ratio": normal_values(splits[2], (TOKENS,), 0.5, 3.0, ((0, 128),), jnp.float32),
        "loss_mask": plant((jax.random.randint(splits[3], (TOKENS,), 0, 4) < 3).astype(jnp.int32), jax.random.fold_in(splits[3], 1), 0, 1),
        "pairs": jax.vmap(lambda own: jax.random.permutation(own, HALF))(jax.random.split(splits[4], N_REP)).reshape((N_REP, HALF)).astype(jnp.int32),
        "inner_w": normal_values(splits[5], (N_REP, D, KVW), 1.0, 6.0, ((0, 4), (1, 32)), jnp.float32),
        "adam_m": normal_values(splits[6], (N_REP, D, KVW), 0.5, 3.0, ((0, 4), (1, 32)), jnp.float32),
        "adam_v": jnp.clip(jnp.exp(math.log(1.0) - 2.9957323 * jax.random.uniform(splits[7], (N_REP, D, KVW), jnp.float32) ** block_scale(splits[7], (N_REP, D, KVW), ((0, 4), (1, 32)), -0.2, 0.2)), 0.05, 1.0),
        "anchor": normal_values(splits[8], (D, KVW), 1.0, 6.0, ((0, 32),), jnp.float32),
        "outer_mom": normal_values(splits[9], (D, KVW), 0.3, 1.75, ((0, 32),), jnp.float32),
    }


dpo_beta = 0.1
decay_one = 0.9
decay_two = 0.95
inner_rate = 0.05
weight_decay = 0.1
epsilon = 1e-08
momentum = 0.9
outer_rate = 0.7

def sequence_weights(ratios, mask_f, partner):
    seq_sums = (ratios * mask_f).reshape(-1, SEQLEN).sum(axis=1)
    half_n = partner.shape[0]
    onehot = (partner[:, None] == jnp.arange(half_n, dtype=jnp.int32)[None, :]).astype(jnp.float32)
    rejected = jnp.dot(onehot, seq_sums[half_n:], precision=lax.Precision.HIGHEST)
    margin = dpo_beta * (seq_sums[:half_n] - rejected)
    pull = jax.nn.sigmoid(-margin)
    push = jnp.dot(pull, onehot, precision=lax.Precision.HIGHEST)
    return jnp.concatenate([-dpo_beta * pull, dpo_beta * push])

def reference(acts, tok_grads, log_ratio, loss_mask, pairs, inner_w, adam_m, adam_v, anchor, outer_mom):
    scale = D ** (-0.5)
    rows = SEQ_DEV * SEQLEN
    group_tok = rows * N_FSDP
    grads_in = []
    moments = []
    delta_total = jnp.zeros((D, KVW), jnp.float32)
    for group in range(N_REP):
        lower = group * group_tok
        upper = lower + group_tok
        x_group = acts[lower:upper]
        mask_f = loss_mask[lower:upper].astype(jnp.float32)
        seq_weight = sequence_weights(log_ratio[lower:upper], mask_f, pairs[group])
        tok_weight = jnp.repeat(seq_weight, SEQLEN) * mask_f
        cot = (tok_weight[:, None] * tok_grads[lower:upper].astype(jnp.float32)).astype(jnp.bfloat16)
        w_half = inner_w[group].astype(jnp.bfloat16)
        grads_in.append((jnp.dot(cot, w_half.T, preferred_element_type=jnp.float32) * scale).astype(jnp.bfloat16))

        def add_block(running, blocks):
            x_block, cot_block = blocks
            term = lax.dot_general(x_block, cot_block, (((0,), (0,)), ((), ())), preferred_element_type=jnp.float32) * scale
            term = lax.optimization_barrier(term.astype(jnp.bfloat16))
            return (running + term.astype(jnp.float32), None)
        grad, _ = lax.scan(add_block, jnp.zeros((D, KVW), jnp.float32), (x_group.reshape(N_FSDP, rows, D), cot.reshape(N_FSDP, rows, KVW)))
        m_next = decay_one * adam_m[group] + (1.0 - decay_one) * grad
        v_next = decay_two * adam_v[group] + (1.0 - decay_two) * grad * grad
        inner_next = inner_w[group] - inner_rate * (m_next / (jnp.sqrt(v_next) + epsilon) + weight_decay * inner_w[group])
        moments.append(m_next)
        delta_total = delta_total + (anchor - inner_next)
    delta_avg = delta_total / N_REP
    new_mom = momentum * outer_mom + delta_avg
    new_anchor = anchor - outer_rate * (delta_avg + momentum * new_mom)
    return (jnp.concatenate(grads_in, axis=0), new_anchor, new_mom, jnp.stack(moments))
```

```python
import functools

import jax
import jax.numpy as jnp
from jax import lax
from jax.experimental import pallas as pl
from jax.experimental.pallas import tpu as pltpu
from jax.sharding import PartitionSpec as P

D = 8192
KVW = 1024
SEQLEN = 256
SEQ_DEV = 2
ROWS = SEQ_DEV * SEQLEN
HALF = 32
SHARD = 256

dpo_beta = 0.1
decay_one = 0.9
decay_two = 0.95
inner_rate = 0.05
weight_decay = 0.1
epsilon = 1e-08
momentum = 0.9
outer_rate = 0.7
SCALE = D ** (-0.5)


def shift(value, dx=0, dz=0, dy=0):
    pairs = []
    for f in range(32):
        x, z, y = f // 8, (f // 2) % 4, f % 2
        pairs.append((f, ((x + dx) % 4) * 8 + ((z + dz) % 4) * 2 + (y + dy) % 2))
    return lax.ppermute(value, "fsdp", pairs)


def swap_rep(value, bit):
    return lax.ppermute(value, "rep", [(r, r ^ bit) for r in range(4)])


def owner(x, z, y):
    return (x % 4) * 8 + (z % 4) * 2 + y


def table(entries):
    return jnp.stack([jnp.asarray(e, jnp.int32) for e in entries])


def cot_kernel(f_ref, v_ref, pairs_ref, mrow_ref, mcol_ref, tg_ref, tgt_ref, cot_ref, cott_ref):
    f = f_ref[0]
    v = v_ref[0:1, :]
    for i in range(1, 4):
        v = v + v_ref[i : i + 1, :]
    row = lax.broadcasted_iota(jnp.int32, (HALF, 128), 0)
    lane = lax.broadcasted_iota(jnp.int32, (HALF, 128), 1)
    onehot = pairs_ref[...] == row
    rejected_col = jnp.sum(jnp.where(lane == row + HALF, v, 0.0), axis=1, keepdims=True)
    rejected = jnp.sum(jnp.where(onehot, rejected_col, 0.0), axis=0, keepdims=True)
    pull = jax.nn.sigmoid(-(dpo_beta * (v - rejected)))
    push = jnp.sum(jnp.where(onehot, pull, 0.0), axis=1, keepdims=True)
    lane_row = lax.broadcasted_iota(jnp.int32, (1, 128), 1)
    row_col = lax.broadcasted_iota(jnp.int32, (HALF, 1), 0)
    weights = []
    for i in range(SEQ_DEV):
        seq = f * SEQ_DEV + i
        chosen = jnp.sum(jnp.where(lane_row == seq, pull, 0.0), axis=1, keepdims=True)
        other = jnp.sum(jnp.where(row_col == seq - HALF, push, 0.0), axis=0, keepdims=True)
        weights.append(jnp.where(seq < HALF, -dpo_beta * chosen, dpo_beta * other))
    tok = lax.broadcasted_iota(jnp.int32, (1, ROWS), 1)
    wrow = jnp.where(tok < SEQLEN, weights[0], weights[1]) * mrow_ref[...]
    cott_ref[...] = (wrow * tgt_ref[...].astype(jnp.float32)).astype(jnp.bfloat16)
    for i in range(SEQ_DEV):
        part = slice(i * SEQLEN, (i + 1) * SEQLEN)
        wcol = weights[i] * mcol_ref[part, :]
        cot_ref[part, :] = (wcol * tg_ref[part, :].astype(jnp.float32)).astype(jnp.bfloat16)


def make_cot(f, v, pairs_pad, mrow, mcol, tg, tgt):
    vmem = pl.BlockSpec(memory_space=pltpu.VMEM)
    return pl.pallas_call(
        cot_kernel,
        out_shape=(
            jax.ShapeDtypeStruct((ROWS, KVW), jnp.bfloat16),
            jax.ShapeDtypeStruct((KVW, ROWS), jnp.bfloat16),
        ),
        in_specs=[pl.BlockSpec(memory_space=pltpu.SMEM)] + [vmem] * 6,
        out_specs=(vmem, vmem),
        cost_estimate=pl.CostEstimate(flops=4_000_000, transcendentals=128, bytes_accessed=4 << 20),
        name="make_cot",
    )(f, v, pairs_pad, mrow, mcol, tg, tgt)


def term(cott_ref, acts_ref):
    return jnp.dot(cott_ref[...], acts_ref[...], preferred_element_type=jnp.float32) * SCALE


def grad_split_kernel(blk, cott_ref, acts_ref, up_ref, down_ref):
    t = term(cott_ref, acts_ref)
    up_ref[...] = t[: KVW // 2].astype(jnp.bfloat16)
    down_ref[...] = t[KVW // 2 :].astype(jnp.bfloat16)


def grad_relay_kernel(upper, blk, cott_ref, acts_ref, add_ref, out_ref):
    t = term(cott_ref, acts_ref)
    add = add_ref[...].astype(jnp.float32)
    h = KVW // 2
    if upper:
        out_ref[:h, :] = (t[:h] + add).astype(jnp.bfloat16)
        out_ref[h:, :] = t[h:].astype(jnp.bfloat16)
    else:
        out_ref[:h, :] = t[:h].astype(jnp.bfloat16)
        out_ref[h:, :] = (t[h:] + add).astype(jnp.bfloat16)


def grad_own_kernel(blk, cott_ref, acts_ref, one_ref, two_ref, *outs):
    t = term(cott_ref, acts_ref)
    t = t + one_ref[...].astype(jnp.float32) + two_ref[...].astype(jnp.float32)
    t = t.astype(jnp.bfloat16)
    for k, out in enumerate(outs):
        @pl.when(pl.program_id(0) == k)
        def _(out=out):
            out[...] = t


COST_GRAD = pl.CostEstimate(
    flops=2 * KVW * ROWS * 4 * SHARD, transcendentals=0, bytes_accessed=6 << 20
)


def grad_call(kernel, blk, cott, acts, adds, add_specs, out_shape, out_specs, name):
    return pl.pallas_call(
        kernel,
        out_shape=out_shape,
        grid_spec=pltpu.PrefetchScalarGridSpec(
            num_scalar_prefetch=1,
            grid=(4,),
            in_specs=[
                pl.BlockSpec((KVW, ROWS), lambda j, b: (0, 0)),
                pl.BlockSpec((ROWS, SHARD), lambda j, b: (0, b[j])),
            ]
            + add_specs,
            out_specs=out_specs,
        ),
        compiler_params=pltpu.CompilerParams(dimension_semantics=("arbitrary",)),
        cost_estimate=COST_GRAD,
        name=name,
    )(blk, cott, acts, *adds)


HALF_SPEC = pl.BlockSpec((KVW // 2, SHARD), lambda j, b: (0, j))
FULL_SPEC = pl.BlockSpec((KVW, SHARD), lambda j, b: (0, j))
HALF_SHAPE = jax.ShapeDtypeStruct((KVW // 2, 4 * SHARD), jnp.bfloat16)
FULL_SHAPE = jax.ShapeDtypeStruct((KVW, 4 * SHARD), jnp.bfloat16)
ONE_SHAPE = jax.ShapeDtypeStruct((KVW, SHARD), jnp.bfloat16)


def grad_split(blk, cott, acts):
    return grad_call(
        grad_split_kernel, blk, cott, acts, [], [], (HALF_SHAPE, HALF_SHAPE), (HALF_SPEC, HALF_SPEC), "grad_split"
    )


def grad_relay(blk, cott, acts, add, upper):
    return grad_call(
        functools.partial(grad_relay_kernel, upper), blk, cott, acts, [add], [HALF_SPEC], FULL_SHAPE, FULL_SPEC, "grad_relay"
    )


def grad_own(blk, cott, acts, one, two):
    whole = pl.BlockSpec((KVW, SHARD), lambda j, b: (0, 0))
    return grad_call(
        grad_own_kernel, blk, cott, acts, [one, two], [FULL_SPEC, FULL_SPEC], (ONE_SHAPE,) * 4, (whole,) * 4, "grad_own"
    )


def input_grad_kernel(blk, cot_ref, w_ref, *rest):
    out_ref = rest[-1]
    t = lax.dot_general(
        cot_ref[...], w_ref[...], (((1,), (1,)), ((), ())), preferred_element_type=jnp.float32
    )
    out_ref[...] = (t * SCALE).astype(jnp.bfloat16)


def input_grad_part(blk, cot, w, previous):
    n = w.shape[0] // SHARD
    aliased = [] if previous is None else [previous]
    return pl.pallas_call(
        input_grad_kernel,
        out_shape=jax.ShapeDtypeStruct((ROWS, D), jnp.bfloat16),
        grid_spec=pltpu.PrefetchScalarGridSpec(
            num_scalar_prefetch=1,
            grid=(n,),
            in_specs=[
                pl.BlockSpec((ROWS, KVW), lambda j, b: (0, 0)),
                pl.BlockSpec((SHARD, KVW), lambda j, b: (j, 0)),
            ]
            + [pl.BlockSpec(memory_space=pl.ANY)] * len(aliased),
            out_specs=pl.BlockSpec((ROWS, SHARD), lambda j, b: (0, b[j])),
        ),
        input_output_aliases={3: 0} if aliased else {},
        compiler_params=pltpu.CompilerParams(dimension_semantics=("arbitrary",)),
        cost_estimate=pl.CostEstimate(
            flops=2 * KVW * ROWS * n * SHARD, transcendentals=0, bytes_accessed=(1 << 20) + n * (3 << 18)
        ),
        name="input_grad",
    )(blk, cot, w, *aliased)


def adam_kernel(keep_ref, recv_ref, m_ref, v_ref, w_ref, anchor_ref, m_out, delta_out):
    grad = (keep_ref[...].astype(jnp.float32) + recv_ref[...].astype(jnp.float32)).T
    w = w_ref[0]
    m_next = decay_one * m_ref[0] + (1.0 - decay_one) * grad
    v_next = decay_two * v_ref[0] + (1.0 - decay_two) * grad * grad
    inner_next = w - inner_rate * (m_next / (jnp.sqrt(v_next) + epsilon) + weight_decay * w)
    m_out[0] = m_next
    delta_out[...] = anchor_ref[...] - inner_next


def adam(keep, recv, m, v, w, anchor):
    col = 256
    gt = pl.BlockSpec((col, SHARD), lambda j: (j, 0))
    cube = pl.BlockSpec((1, SHARD, col), lambda j: (0, 0, j))
    flat = pl.BlockSpec((SHARD, col), lambda j: (0, j))
    return pl.pallas_call(
        adam_kernel,
        grid=(KVW // col,),
        out_shape=(
            jax.ShapeDtypeStruct((1, SHARD, KVW), jnp.float32),
            jax.ShapeDtypeStruct((SHARD, KVW), jnp.float32),
        ),
        in_specs=[gt, gt, cube, cube, cube, flat],
        out_specs=(cube, flat),
        cost_estimate=pl.CostEstimate(flops=20 << 18, transcendentals=2 << 18, bytes_accessed=7 << 20),
        name="adam",
    )(keep, recv, m, v, w, anchor)


def local(acts, tok_grads, log_ratio, loss_mask, pairs, inner_w, adam_m, adam_v, anchor, outer_mom):
    f = lax.axis_index("fsdp")
    mx, mz, my = f // 8, (f // 2) % 4, f % 2
    core = lax.axis_index("rep") % 2

    mask_f = loss_mask.astype(jnp.float32)
    own_sums = (log_ratio * mask_f).reshape(SEQ_DEV, SEQLEN).sum(axis=1)
    lane = lax.broadcasted_iota(jnp.int32, (1, 128), 1)
    row = jnp.where(lane == 2 * f, own_sums[0], jnp.where(lane == 2 * f + 1, own_sums[1], 0.0))
    row = row + shift(row, dy=1)
    row = row + shift(row, dx=1) + shift(row, dx=-1) + shift(row, dx=2)
    rows = jnp.concatenate([row, shift(row, dz=1), shift(row, dz=-1), shift(row, dz=2)], axis=0)

    w_half = inner_w[0].astype(jnp.bfloat16)
    w_other = shift(w_half, dy=1)
    first = jnp.where(my == 0, w_half, w_other)
    second = jnp.where(my == 0, w_other, w_half)
    near0 = jnp.concatenate([first, shift(first, dx=-1), shift(first, dx=2), shift(first, dx=1)], axis=0)
    near1 = jnp.concatenate([second, shift(second, dz=-1), shift(second, dz=2), shift(second, dz=1)], axis=0)

    pairs_pad = jnp.pad(pairs, ((0, 0), (0, 128 - HALF)), constant_values=-1)
    cot, cott = make_cot(
        f.reshape(1).astype(jnp.int32), rows, pairs_pad, mask_f.reshape(1, ROWS), mask_f.reshape(ROWS, 1),
        tok_grads, tok_grads.T,
    )

    def blk(colour, k):
        if colour == 0:
            return table([owner(mx + k, mz + j, 0) for j in range(4)])
        return table([owner(mx + j, mz + k, 1) for j in range(4)])

    def big(colour, value, step):
        return shift(value, dx=step) if colour == 0 else shift(value, dz=step)

    def small(colour, value, step):
        return shift(value, dz=step) if colour == 0 else shift(value, dx=step)

    sums = []
    relays = []
    for c in (0, 1):
        up, down = grad_split(blk(c, 2), cott, acts)
        relays.append((big(c, up, 1), big(c, down, -1)))
    sent = []
    for c in (0, 1):
        up, down = relays[c]
        plus = big(c, grad_relay(blk(c, 1), cott, acts, up, True), 1)
        minus = big(c, grad_relay(blk(c, 3), cott, acts, down, False), -1)
        sent.append((plus, minus))
    for c in (0, 1):
        parts = grad_own(blk(c, 0), cott, acts, *sent[c])
        total = parts[0].astype(jnp.float32)
        for k, step in ((1, 1), (2, 2), (3, -1)):
            total = total + small(c, parts[k], step).astype(jnp.float32)
        sums.append(total.astype(jnp.bfloat16))
    keep = jnp.where(my == 0, sums[0], sums[1])
    give = jnp.where(my == 0, sums[1], sums[0])
    new_m, delta = adam(keep, shift(give, dy=1), adam_m, adam_v, inner_w, anchor)

    h = SHARD // 2
    mine = jnp.where(core == 0, delta[:h], delta[h:])
    other = jnp.where(core == 0, delta[h:], delta[:h])
    mine = mine + swap_rep(other, 1)
    mine = mine + swap_rep(mine, 2)
    other = swap_rep(mine, 1)
    total = jnp.concatenate([jnp.where(core == 0, mine, other), jnp.where(core == 0, other, mine)], axis=0)
    delta_avg = total / 4
    new_mom = momentum * outer_mom + delta_avg
    new_anchor = anchor - outer_rate * (delta_avg + momentum * new_mom)

    def cols(colour, k, ks):
        if colour == 0:
            return table([owner(mx + j, mz + k, 0) for j in ks])
        return table([owner(mx + k, mz + j, 1) for j in ks])

    every = range(4)
    nears = (near0, near1)
    out = None
    far = []
    for c in (0, 1):
        far.append((small(c, nears[c], -1), small(c, nears[c], 1)))
    for c in (0, 1):
        out = input_grad_part(cols(c, 0, every), cot, nears[c], out)
    last = []
    for c in (0, 1):
        plus, minus = far[c]
        last.append((small(c, plus[: 2 * SHARD], -1), small(c, minus[2 * SHARD :], 1)))
        out = input_grad_part(cols(c, 1, every), cot, plus, out)
        out = input_grad_part(cols(c, 3, every), cot, minus, out)
    for c in (0, 1):
        out = input_grad_part(cols(c, 2, (0, 1)), cot, last[c][0], out)
        out = input_grad_part(cols(c, 2, (2, 3)), cot, last[c][1], out)
    return (out, new_anchor, new_mom, new_m)


def solution(mesh):
    return jax.shard_map(
        local,
        mesh=mesh,
        in_specs=(
            P(("rep", "fsdp"), None),
            P(("rep", "fsdp"), None),
            P(("rep", "fsdp")),
            P(("rep", "fsdp")),
            P("rep", None),
            P("rep", "fsdp", None),
            P("rep", "fsdp", None),
            P("rep", "fsdp", None),
            P("fsdp", None),
            P("fsdp", None),
        ),
        out_specs=(
            P(("rep", "fsdp"), None),
            P("fsdp", None),
            P("fsdp", None),
            P("rep", "fsdp", None),
        ),
        check_vma=False,
    )
```

```python
import functools

import jax
import jax.numpy as jnp
from jax import lax
from jax.experimental import pallas as pl
from jax.experimental.pallas import tpu as pltpu
from jax.sharding import PartitionSpec as P


D = 8192
KVW = 1024
SEQLEN = 256
SEQ_DEV = 2
ROWS = SEQ_DEV * SEQLEN
HALF = 32
SHARD = 256

dpo_beta = 0.1
decay_one = 0.9
decay_two = 0.95
inner_rate = 0.05
weight_decay = 0.1
epsilon = 1e-08
momentum = 0.9
outer_rate = 0.7
SCALE = D ** (-0.5)


GRANT = 24 << 20


def send(value, target):
    pairs = []
    for f in range(32):
        x, z, y = target(f // 8, (f // 2) % 4, f % 2)
        pairs.append((f, (x % 4) * 8 + (z % 4) * 2 + y % 2))
    return lax.ppermute(value, "fsdp", pairs)


def shift(value, dx=0, dz=0, dy=0):
    return send(value, lambda x, z, y: (x + dx, z + dz, y + dy))


def send_tilted(value, step, far):
    pairs = []
    for i in range(128):
        rep, f = i // 32, i % 32
        x, z, y = f // 8, (f // 2) % 4, f % 2
        if (rep + y + far) % 2:
            z = (z + step) % 4
        else:
            x = (x + step) % 4
        pairs.append((i, rep * 32 + x * 8 + z * 2 + y))
    return lax.ppermute(value, ("rep", "fsdp"), pairs)


def shift_near(value, step):
    return send_tilted(value, step, 0)


def shift_far(value, step):
    return send_tilted(value, step, 1)


def swap_rep(value, bit):
    return lax.ppermute(value, "rep", [(r, r ^ bit) for r in range(4)])


def owner(x, z, y):
    return (x % 4) * 8 + (z % 4) * 2 + y


def sums_kernel(f_ref, ratio_ref, mask_ref, row_ref):
    kept = ratio_ref[...] * mask_ref[...].astype(jnp.float32)
    lane = lax.broadcasted_iota(jnp.int32, (1, 128), 1)
    row = jnp.zeros((1, 128), jnp.float32)
    rows = kept.shape[0] // SEQ_DEV
    for i in range(SEQ_DEV):
        part = jnp.sum(kept[i * rows : (i + 1) * rows], axis=0, keepdims=True)
        part = jnp.sum(part, axis=1, keepdims=True)
        row = jnp.where(lane == f_ref[0] * SEQ_DEV + i, part, row)
    row_ref[...] = row


def seq_sums(f, ratio, mask):
    vmem = pl.BlockSpec(memory_space=pltpu.VMEM)
    return pl.pallas_call(
        sums_kernel,
        out_shape=jax.ShapeDtypeStruct((1, 128), jnp.float32),
        in_specs=[pl.BlockSpec(memory_space=pltpu.SMEM), vmem, vmem],
        out_specs=vmem,
        compiler_params=pltpu.CompilerParams(vmem_limit_bytes=1 << 20),
        cost_estimate=pl.CostEstimate(flops=2048, transcendentals=0, bytes_accessed=4096),
        name="seq_sums",
    )(f, ratio, mask)


def cot_kernel(f_ref, v0_ref, v1_ref, v2_ref, v3_ref, pairs_ref, mrow_ref, mcol_ref, tg_ref, tgt_ref, cot_ref, cott_ref):
    f = f_ref[0]
    v = v0_ref[...] + v1_ref[...] + v2_ref[...] + v3_ref[...]
    row = lax.broadcasted_iota(jnp.int32, (HALF, 128), 0)
    lane = lax.broadcasted_iota(jnp.int32, (HALF, 128), 1)
    onehot = pairs_ref[...] == row
    rejected_col = jnp.sum(jnp.where(lane == row + HALF, v, 0.0), axis=1, keepdims=True)
    rejected = jnp.sum(jnp.where(onehot, rejected_col, 0.0), axis=0, keepdims=True)
    pull = jax.nn.sigmoid(-(dpo_beta * (v - rejected)))
    push = jnp.sum(jnp.where(onehot, pull, 0.0), axis=1, keepdims=True)
    lane_row = lax.broadcasted_iota(jnp.int32, (1, 128), 1)
    row_col = lax.broadcasted_iota(jnp.int32, (HALF, 1), 0)
    weights = []
    for i in range(SEQ_DEV):
        seq = f * SEQ_DEV + i
        chosen = jnp.sum(jnp.where(lane_row == seq, pull, 0.0), axis=1, keepdims=True)
        other = jnp.sum(jnp.where(row_col == seq - HALF, push, 0.0), axis=0, keepdims=True)
        weights.append(jnp.where(seq < HALF, -dpo_beta * chosen, dpo_beta * other))
    tok = lax.broadcasted_iota(jnp.int32, (1, ROWS), 1)
    wrow = jnp.where(tok < SEQLEN, weights[0], weights[1]) * mrow_ref[...]
    cott_ref[...] = (wrow * tgt_ref[...].astype(jnp.float32)).astype(jnp.bfloat16)
    for i in range(SEQ_DEV):
        part = slice(i * SEQLEN, (i + 1) * SEQLEN)
        wcol = weights[i] * mcol_ref[part, :]
        cot_ref[part, :] = (wcol * tg_ref[part, :].astype(jnp.float32)).astype(jnp.bfloat16)


def make_cot(f, rows, pairs_pad, mrow, mcol, tg, tgt):
    vmem = pl.BlockSpec(memory_space=pltpu.VMEM)
    return pl.pallas_call(
        cot_kernel,
        out_shape=(
            jax.ShapeDtypeStruct((ROWS, KVW), jnp.bfloat16),
            jax.ShapeDtypeStruct((KVW, ROWS), jnp.bfloat16),
        ),
        in_specs=[pl.BlockSpec(memory_space=pltpu.SMEM)] + [vmem] * 9,
        out_specs=(vmem, vmem),
        compiler_params=pltpu.CompilerParams(vmem_limit_bytes=GRANT),
        cost_estimate=pl.CostEstimate(flops=4_000_000, transcendentals=128, bytes_accessed=4 << 20),
        name="make_cot",
    )(f, *rows, pairs_pad, mrow, mcol, tg, tgt)


def term(cott_ref, acts_refs):
    acts = jnp.concatenate([a[...] for a in acts_refs], axis=1)
    return jnp.dot(cott_ref[...], acts, preferred_element_type=jnp.float32) * SCALE


def split_kernel(tab, cott_ref, a0, a1, *outs):
    t = term(cott_ref, (a0, a1)).astype(jnp.bfloat16)
    for colour in range(2):
        @pl.when(pl.program_id(0) // 2 == colour)
        def _(colour=colour):
            outs[2 * colour][...] = t[: KVW // 2]
            outs[2 * colour + 1][...] = t[KVW // 2 :]


def rest_kernel(tab, cott_ref, a0, a1, *outs):
    t = term(cott_ref, (a0, a1)).astype(jnp.bfloat16)
    for i, out in enumerate(outs):
        @pl.when(pl.program_id(0) // 2 == i)
        def _(out=out):
            out[...] = t


def products(kernel, first, count, rows, split, tab, cott, acts):
    spec = [
        pl.BlockSpec((rows, 2 * SHARD), lambda s, b, i=i: (0, jnp.clip(s - 2 * i, 0, 1)))
        for i in range(count)
        for _ in range(split)
    ]
    return pl.pallas_call(
        kernel,
        out_shape=(jax.ShapeDtypeStruct((rows, 4 * SHARD), jnp.bfloat16),) * (count * split),
        grid_spec=pltpu.PrefetchScalarGridSpec(
            num_scalar_prefetch=1,
            grid=(2 * count,),
            in_specs=[
                pl.BlockSpec((KVW, ROWS), lambda s, b: (0, 0)),
                pl.BlockSpec((ROWS, SHARD), lambda s, b: (0, b[first + 2 * s])),
                pl.BlockSpec((ROWS, SHARD), lambda s, b: (0, b[first + 2 * s + 1])),
            ],
            out_specs=tuple(spec),
        ),
        compiler_params=pltpu.CompilerParams(
            dimension_semantics=("arbitrary",), vmem_limit_bytes=GRANT
        ),
        cost_estimate=pl.CostEstimate(
            flops=2 * KVW * ROWS * 4 * SHARD * count, transcendentals=0, bytes_accessed=count * (3 << 20)
        ),
    )(tab, cott, acts, acts)


def input_grad_kernel(edges, tab, cot_ref, *rest):
    out_ref = rest[-1]
    for i, (low, high) in enumerate(edges):
        @pl.when((pl.program_id(0) >= low) & (pl.program_id(0) < high))
        def _(w_ref=rest[i]):
            t = lax.dot_general(
                cot_ref[...], w_ref[...], (((1,), (1,)), ((), ())), preferred_element_type=jnp.float32
            )
            out_ref[...] = (t * SCALE).astype(jnp.bfloat16)


def input_grad_part(first, tab, cot, pieces, previous):
    edges, n = [], 0
    for piece in pieces:
        edges.append((n, n + piece.shape[0] // SHARD))
        n = edges[-1][1]
    aliased = [] if previous is None else [previous]
    return pl.pallas_call(
        functools.partial(input_grad_kernel, tuple(edges)),
        out_shape=jax.ShapeDtypeStruct((ROWS, D), jnp.bfloat16),
        grid_spec=pltpu.PrefetchScalarGridSpec(
            num_scalar_prefetch=1,
            grid=(n,),
            in_specs=[pl.BlockSpec((ROWS, KVW), lambda s, b: (0, 0))]
            + [
                pl.BlockSpec((SHARD, KVW), lambda s, b, e=e: (jnp.clip(s - e[0], 0, e[1] - e[0] - 1), 0))
                for e in edges
            ]
            + [pl.BlockSpec(memory_space=pl.ANY)] * len(aliased),
            out_specs=pl.BlockSpec((ROWS, SHARD), lambda s, b: (0, b[first + s])),
        ),
        input_output_aliases={2 + len(pieces): 0} if aliased else {},
        compiler_params=pltpu.CompilerParams(
            dimension_semantics=("arbitrary",), vmem_limit_bytes=GRANT
        ),
        cost_estimate=pl.CostEstimate(
            flops=2 * KVW * ROWS * n * SHARD, transcendentals=0, bytes_accessed=(1 << 20) + n * (3 << 18)
        ),
        name="input_grad",
    )(tab, cot, *pieces, *aliased)


def choose_kernel(my_ref, *refs):
    first, second = [
        sum(r[...].astype(jnp.float32) for r in refs[4 * c : 4 * c + 4]).astype(jnp.bfloat16) for c in (0, 1)
    ]
    keep_ref, give_ref = refs[8:]
    upper = my_ref[0] == 1
    keep_ref[...] = jnp.where(upper, second, first)
    give_ref[...] = jnp.where(upper, first, second)


def choose(my, parts):
    block = pl.BlockSpec((256, SHARD), lambda i: (i, 0))
    return pl.pallas_call(
        choose_kernel,
        grid=(KVW // 256,),
        out_shape=(jax.ShapeDtypeStruct((KVW, SHARD), jnp.bfloat16),) * 2,
        in_specs=[pl.BlockSpec(memory_space=pltpu.SMEM)] + [block] * 8,
        out_specs=(block, block),
        compiler_params=pltpu.CompilerParams(vmem_limit_bytes=GRANT),
        cost_estimate=pl.CostEstimate(flops=2 << 20, transcendentals=0, bytes_accessed=5 << 20),
        name="choose",
    )(my, *parts)


def adam_kernel(keep_ref, recv_ref, m_ref, v_ref, w_ref, anchor_ref, m_out, delta_out):
    grad = (keep_ref[...].astype(jnp.float32) + recv_ref[...].astype(jnp.float32)).T
    w = w_ref[0]
    m_next = decay_one * m_ref[0] + (1.0 - decay_one) * grad
    v_next = decay_two * v_ref[0] + (1.0 - decay_two) * grad * grad
    inner_next = w - inner_rate * (m_next / (jnp.sqrt(v_next) + epsilon) + weight_decay * w)
    m_out[0] = m_next
    delta_out[...] = anchor_ref[...] - inner_next


def adam(keep, recv, m, v, w, anchor):
    col = 128
    gt = pl.BlockSpec((col, SHARD), lambda j: (j, 0))
    cube = pl.BlockSpec((1, SHARD, col), lambda j: (0, 0, j))
    flat = pl.BlockSpec((SHARD, col), lambda j: (0, j))
    return pl.pallas_call(
        adam_kernel,
        grid=(KVW // col,),
        out_shape=(
            jax.ShapeDtypeStruct((1, SHARD, KVW), jnp.float32),
            jax.ShapeDtypeStruct((SHARD, KVW), jnp.float32),
        ),
        in_specs=[gt, gt, cube, cube, cube, flat],
        out_specs=(cube, flat),
        compiler_params=pltpu.CompilerParams(vmem_limit_bytes=GRANT),
        cost_estimate=pl.CostEstimate(flops=20 << 18, transcendentals=2 << 18, bytes_accessed=7 << 20),
        name="adam",
    )(keep, recv, m, v, w, anchor)


def local(acts, tok_grads, log_ratio, loss_mask, pairs, inner_w, adam_m, adam_v, anchor, outer_mom):
    f = lax.axis_index("fsdp")
    mx, mz, my = f // 8, (f // 2) % 4, f % 2
    core = lax.axis_index("rep") % 2
    bf16, f32 = jnp.bfloat16, jnp.float32

    in_hbm = lambda value: pltpu.with_memory_space_constraint(value, pltpu.HBM)
    acts = in_hbm(acts)

    def far0(k):
        return [owner(mx + k, mz + j, 0) for j in range(4)]

    def far1(k):
        return [owner(mx + j, mz + k, 1) for j in range(4)]

    tilt = (core + my) % 2

    def gathered(who, k, js):
        axis, plane = (tilt, my) if who == "own" else (1 - tilt, 1 - my)
        return [
            jnp.where(axis == 0, owner(mx + j, mz + k, plane), owner(mx + k, mz + j, plane)) for j in js
        ]

    entries = far0(2) + far1(2) + far0(1) + far0(3) + far1(1) + far1(3) + far0(0) + far1(0)
    starts = []
    every, low, high = range(4), (0, 1), (2, 3)
    for group in (
        [("own", 0, every), ("oth", 0, every), ("own", 1, high), ("own", 3, low)],
        [("own", 1, low), ("own", 3, high), ("oth", 1, high), ("oth", 3, low)],
        [("oth", 1, low), ("oth", 3, high), ("own", 2, every)],
        [("oth", 2, every)],
    ):
        starts.append(len(entries))
        for entry in group:
            entries = entries + gathered(*entry)
    tab = jnp.stack(entries).astype(jnp.int32)

    mask_f = loss_mask.astype(f32)
    where_f = f.reshape(1).astype(jnp.int32)
    row = seq_sums(where_f, log_ratio.reshape(ROWS // 128, 128), loss_mask.reshape(ROWS // 128, 128))
    row = row + shift(row, dy=1)
    row = row + shift(row, dx=1) + shift(row, dx=-1) + shift(row, dx=2)
    rows = (row, shift(row, dz=1), shift(row, dz=-1), shift(row, dz=2))

    w_half = inner_w[0].astype(bf16)
    one, two, three = shift_near(w_half, -1), shift_near(w_half, 2), shift_near(w_half, 1)
    row_low = jnp.concatenate([w_half, one], axis=0)
    row_high = jnp.concatenate([two, three], axis=0)
    other_low, other_high = shift(row_low, dy=1), shift(row_high, dy=1)
    next_high, prev_low = shift_far(row_high, -1), shift_far(row_low, 1)
    next_low, prev_high = shift_far(row_low, -1), shift_far(row_high, 1)
    rest = (shift(next_high, dy=1), shift(prev_low, dy=1))
    relay = (shift_far(next_low, -1), shift_far(prev_high, 1))
    cross = (shift_near(other_low, -1), shift_near(other_high, 1))
    last = (shift_near(cross[0], -1), shift_near(cross[1], 1))

    pairs_pad = jnp.pad(pairs, ((0, 0), (0, 128 - HALF)), constant_values=-1)
    cot, cott = make_cot(
        where_f, rows, pairs_pad, mask_f.reshape(1, ROWS), mask_f.reshape(ROWS, 1),
        tok_grads, tok_grads.T,
    )

    def big(colour, value, step):
        return shift(value, dx=step) if colour == 0 else shift(value, dz=step)

    def small(colour, value, step):
        return shift(value, dz=step) if colour == 0 else shift(value, dx=step)

    h = KVW // 2
    ups = products(split_kernel, 0, 2, h, 2, tab, cott, acts)
    terms = products(rest_kernel, 8, 6, KVW, 1, tab, cott, acts)
    sums = []
    relayed = []
    for c in (0, 1):
        relayed.append((big(c, ups[2 * c], 1), big(c, ups[2 * c + 1], -1)))
    got = []
    for c in (0, 1):
        plus = terms[2 * c].at[:h].add(relayed[c][0])
        minus = terms[2 * c + 1].at[h:].add(relayed[c][1])
        got.append((big(c, plus, 1), big(c, minus, -1)))
    for c in (0, 1):
        parts = []
        for k in range(4):
            cols = slice(k * SHARD, (k + 1) * SHARD)
            part = terms[4 + c][:, cols].astype(f32)
            part = part + got[c][0][:, cols].astype(f32) + got[c][1][:, cols].astype(f32)
            parts.append(part.astype(bf16))
        moved = [small(c, parts[k], step) for k, step in ((1, 1), (2, 2), (3, -1))]
        sums += [parts[0]] + moved
    keep, give = choose(my.reshape(1).astype(jnp.int32), sums)
    recv = in_hbm(shift(in_hbm(give), dy=1))
    new_m, delta = adam(keep, recv, in_hbm(adam_m), in_hbm(adam_v), in_hbm(inner_w), in_hbm(anchor))

    hs = SHARD // 2
    part = jnp.where(core == 0, delta[:hs], delta[hs:])
    other = jnp.where(core == 0, delta[hs:], delta[:hs])
    part = part + swap_rep(other, 1)
    part = part + swap_rep(part, 2)
    other = swap_rep(part, 1)
    total = jnp.concatenate([jnp.where(core == 0, part, other), jnp.where(core == 0, other, part)], axis=0)
    delta_avg = total / 4
    new_mom = momentum * outer_mom + delta_avg
    new_anchor = anchor - outer_rate * (delta_avg + momentum * new_mom)

    groups = (
        (row_low, row_high, other_low, other_high, next_high, prev_low),
        (next_low, prev_high) + rest,
        cross + relay,
        last,
    )
    out = None
    for i, group in enumerate(groups):
        out = input_grad_part(starts[i], tab, cot, group, out)
    return (out, new_anchor, new_mom, new_m)


def solution(mesh):
    return jax.shard_map(
        local,
        mesh=mesh,
        in_specs=(
            P(("rep", "fsdp"), None),
            P(("rep", "fsdp"), None),
            P(("rep", "fsdp")),
            P(("rep", "fsdp")),
            P("rep", None),
            P("rep", "fsdp", None),
            P("rep", "fsdp", None),
            P("rep", "fsdp", None),
            P("fsdp", None),
            P("fsdp", None),
        ),
        out_specs=(
            P(("rep", "fsdp"), None),
            P("fsdp", None),
            P("fsdp", None),
            P("rep", "fsdp", None),
        ),
        check_vma=False,
    )
```

```python
import functools

import jax
import jax.numpy as jnp
from jax import lax
from jax.experimental import pallas as pl
from jax.experimental.pallas import tpu as pltpu
from jax.sharding import PartitionSpec as P


D = 8192
KVW = 1024
SEQLEN = 256
SEQ_DEV = 2
ROWS = SEQ_DEV * SEQLEN
HALF = 32
SHARD = 256

dpo_beta = 0.1
decay_one = 0.9
decay_two = 0.95
inner_rate = 0.05
weight_decay = 0.1
epsilon = 1e-08
momentum = 0.9
outer_rate = 0.7
SCALE = D ** (-0.5)


GRANT = 24 << 20


def send(value, target):
    pairs = []
    for f in range(32):
        x, z, y = target(f // 8, (f // 2) % 4, f % 2)
        pairs.append((f, (x % 4) * 8 + (z % 4) * 2 + y % 2))
    return lax.ppermute(value, "fsdp", pairs)


def shift(value, dx=0, dz=0, dy=0):
    return send(value, lambda x, z, y: (x + dx, z + dz, y + dy))


def send_tilted(value, step, far):
    pairs = []
    for i in range(128):
        rep, f = i // 32, i % 32
        x, z, y = f // 8, (f // 2) % 4, f % 2
        if (rep + y + far) % 2:
            z = (z + step) % 4
        else:
            x = (x + step) % 4
        pairs.append((i, rep * 32 + x * 8 + z * 2 + y))
    return lax.ppermute(value, ("rep", "fsdp"), pairs)


def shift_near(value, step):
    return send_tilted(value, step, 0)


def shift_far(value, step):
    return send_tilted(value, step, 1)


def swap_rep(value, bit):
    return lax.ppermute(value, "rep", [(r, r ^ bit) for r in range(4)])


def owner(x, z, y):
    return (x % 4) * 8 + (z % 4) * 2 + y


def sums_kernel(f_ref, ratio_ref, mask_ref, row_ref):
    kept = ratio_ref[...] * mask_ref[...].astype(jnp.float32)
    lane = lax.broadcasted_iota(jnp.int32, (1, 128), 1)
    row = jnp.zeros((1, 128), jnp.float32)
    rows = kept.shape[0] // SEQ_DEV
    for i in range(SEQ_DEV):
        part = jnp.sum(kept[i * rows : (i + 1) * rows], axis=0, keepdims=True)
        part = jnp.sum(part, axis=1, keepdims=True)
        row = jnp.where(lane == f_ref[0] * SEQ_DEV + i, part, row)
    row_ref[...] = row


def seq_sums(f, ratio, mask):
    vmem = pl.BlockSpec(memory_space=pltpu.VMEM)
    return pl.pallas_call(
        sums_kernel,
        out_shape=jax.ShapeDtypeStruct((1, 128), jnp.float32),
        in_specs=[pl.BlockSpec(memory_space=pltpu.SMEM), vmem, vmem],
        out_specs=vmem,
        compiler_params=pltpu.CompilerParams(vmem_limit_bytes=1 << 20),
        cost_estimate=pl.CostEstimate(flops=2048, transcendentals=0, bytes_accessed=4096),
        name="seq_sums",
    )(f, ratio, mask)


def cot_kernel(f_ref, v0_ref, v1_ref, v2_ref, v3_ref, pairs_ref, mrow_ref, mcol_ref, tg_ref, tgt_ref, cot_ref, cott_ref):
    f = f_ref[0]
    v = v0_ref[...] + v1_ref[...] + v2_ref[...] + v3_ref[...]
    row = lax.broadcasted_iota(jnp.int32, (HALF, 128), 0)
    lane = lax.broadcasted_iota(jnp.int32, (HALF, 128), 1)
    onehot = pairs_ref[...] == row
    rejected_col = jnp.sum(jnp.where(lane == row + HALF, v, 0.0), axis=1, keepdims=True)
    rejected = jnp.sum(jnp.where(onehot, rejected_col, 0.0), axis=0, keepdims=True)
    pull = jax.nn.sigmoid(-(dpo_beta * (v - rejected)))
    push = jnp.sum(jnp.where(onehot, pull, 0.0), axis=1, keepdims=True)
    lane_row = lax.broadcasted_iota(jnp.int32, (1, 128), 1)
    row_col = lax.broadcasted_iota(jnp.int32, (HALF, 1), 0)
    weights = []
    for i in range(SEQ_DEV):
        seq = f * SEQ_DEV + i
        chosen = jnp.sum(jnp.where(lane_row == seq, pull, 0.0), axis=1, keepdims=True)
        other = jnp.sum(jnp.where(row_col == seq - HALF, push, 0.0), axis=0, keepdims=True)
        weights.append(jnp.where(seq < HALF, -dpo_beta * chosen, dpo_beta * other))
    tok = lax.broadcasted_iota(jnp.int32, (1, ROWS), 1)
    wrow = jnp.where(tok < SEQLEN, weights[0], weights[1]) * mrow_ref[...].astype(jnp.float32)
    cott_ref[...] = (wrow * tgt_ref[...].astype(jnp.float32)).astype(jnp.bfloat16)
    for i in range(SEQ_DEV):
        part = slice(i * SEQLEN, (i + 1) * SEQLEN)
        wcol = weights[i] * mcol_ref[part, :].astype(jnp.float32)
        cot_ref[part, :] = (wcol * tg_ref[part, :].astype(jnp.float32)).astype(jnp.bfloat16)


def make_cot(f, rows, pairs_pad, mrow, mcol, tg, tgt):
    vmem = pl.BlockSpec(memory_space=pltpu.VMEM)
    return pl.pallas_call(
        cot_kernel,
        out_shape=(
            jax.ShapeDtypeStruct((ROWS, KVW), jnp.bfloat16),
            jax.ShapeDtypeStruct((KVW, ROWS), jnp.bfloat16),
        ),
        in_specs=[pl.BlockSpec(memory_space=pltpu.SMEM)] + [vmem] * 9,
        out_specs=(vmem, vmem),
        compiler_params=pltpu.CompilerParams(vmem_limit_bytes=GRANT),
        cost_estimate=pl.CostEstimate(flops=4_000_000, transcendentals=128, bytes_accessed=4 << 20),
        name="make_cot",
    )(f, *rows, pairs_pad, mrow, mcol, tg, tgt)


def term(cott_ref, acts_refs):
    acts = jnp.concatenate([a[...] for a in acts_refs], axis=1)
    return jnp.dot(cott_ref[...], acts, preferred_element_type=jnp.float32) * SCALE


def split_kernel(tab, cott_ref, a0, a1, *outs):
    t = term(cott_ref, (a0, a1)).astype(jnp.bfloat16)
    for colour in range(2):
        @pl.when(pl.program_id(0) // 2 == colour)
        def _(colour=colour):
            outs[2 * colour][...] = t[: KVW // 2]
            outs[2 * colour + 1][...] = t[KVW // 2 :]


def rest_kernel(tab, cott_ref, a0, a1, *outs):
    t = term(cott_ref, (a0, a1)).astype(jnp.bfloat16)
    for i, out in enumerate(outs):
        @pl.when(pl.program_id(0) // 2 == i)
        def _(out=out):
            out[...] = t


def products(kernel, first, count, rows, split, tab, cott, acts):
    spec = [
        pl.BlockSpec((rows, 2 * SHARD), lambda s, b, i=i: (0, jnp.clip(s - 2 * i, 0, 1)))
        for i in range(count)
        for _ in range(split)
    ]
    return pl.pallas_call(
        kernel,
        out_shape=(jax.ShapeDtypeStruct((rows, 4 * SHARD), jnp.bfloat16),) * (count * split),
        grid_spec=pltpu.PrefetchScalarGridSpec(
            num_scalar_prefetch=1,
            grid=(2 * count,),
            in_specs=[
                pl.BlockSpec((KVW, ROWS), lambda s, b: (0, 0)),
                pl.BlockSpec((ROWS, SHARD), lambda s, b: (0, b[first + 2 * s])),
                pl.BlockSpec((ROWS, SHARD), lambda s, b: (0, b[first + 2 * s + 1])),
            ],
            out_specs=tuple(spec),
        ),
        compiler_params=pltpu.CompilerParams(
            dimension_semantics=("arbitrary",), vmem_limit_bytes=GRANT
        ),
        cost_estimate=pl.CostEstimate(
            flops=2 * KVW * ROWS * 4 * SHARD * count, transcendentals=0, bytes_accessed=count * (3 << 20)
        ),
    )(tab, cott, acts, acts)


def input_grad_kernel(edges, tab, cot_ref, *rest):
    out_ref = rest[-1]
    for i, (low, high) in enumerate(edges):
        @pl.when((pl.program_id(0) >= low) & (pl.program_id(0) < high))
        def _(w_ref=rest[i]):
            t = lax.dot_general(
                cot_ref[...], w_ref[...], (((1,), (1,)), ((), ())), preferred_element_type=jnp.float32
            )
            out_ref[...] = (t * SCALE).astype(jnp.bfloat16)


def input_grad_part(first, tab, cot, pieces, previous):
    edges, n = [], 0
    for piece in pieces:
        edges.append((n, n + piece.shape[0] // SHARD))
        n = edges[-1][1]
    aliased = [] if previous is None else [previous]
    return pl.pallas_call(
        functools.partial(input_grad_kernel, tuple(edges)),
        out_shape=jax.ShapeDtypeStruct((ROWS, D), jnp.bfloat16),
        grid_spec=pltpu.PrefetchScalarGridSpec(
            num_scalar_prefetch=1,
            grid=(n,),
            in_specs=[pl.BlockSpec((ROWS, KVW), lambda s, b: (0, 0))]
            + [
                pl.BlockSpec((SHARD, KVW), lambda s, b, e=e: (jnp.clip(s - e[0], 0, e[1] - e[0] - 1), 0))
                for e in edges
            ]
            + [pl.BlockSpec(memory_space=pl.ANY)] * len(aliased),
            out_specs=pl.BlockSpec((ROWS, SHARD), lambda s, b: (0, b[first + s])),
        ),
        input_output_aliases={2 + len(pieces): 0} if aliased else {},
        compiler_params=pltpu.CompilerParams(
            dimension_semantics=("arbitrary",), vmem_limit_bytes=GRANT
        ),
        cost_estimate=pl.CostEstimate(
            flops=2 * KVW * ROWS * n * SHARD, transcendentals=0, bytes_accessed=(1 << 20) + n * (3 << 18)
        ),
        name="input_grad",
    )(tab, cot, *pieces, *aliased)


def choose_kernel(my_ref, *refs):
    first, second = [
        sum(r[...].astype(jnp.float32) for r in refs[4 * c : 4 * c + 4]).astype(jnp.bfloat16) for c in (0, 1)
    ]
    keep_ref, give_ref = refs[8:]
    upper = my_ref[0] == 1
    keep_ref[...] = jnp.where(upper, second, first)
    give_ref[...] = jnp.where(upper, first, second)


def choose(my, parts):
    block = pl.BlockSpec((256, SHARD), lambda i: (i, 0))
    return pl.pallas_call(
        choose_kernel,
        grid=(KVW // 256,),
        out_shape=(jax.ShapeDtypeStruct((KVW, SHARD), jnp.bfloat16),) * 2,
        in_specs=[pl.BlockSpec(memory_space=pltpu.SMEM)] + [block] * 8,
        out_specs=(block, block),
        compiler_params=pltpu.CompilerParams(vmem_limit_bytes=GRANT),
        cost_estimate=pl.CostEstimate(flops=2 << 20, transcendentals=0, bytes_accessed=5 << 20),
        name="choose",
    )(my, *parts)


def adam_kernel(keep_ref, recv_ref, m_ref, v_ref, w_ref, anchor_ref, m_out, delta_out):
    grad = (keep_ref[...].astype(jnp.float32) + recv_ref[...].astype(jnp.float32)).T
    w = w_ref[0]
    m_next = decay_one * m_ref[0] + (1.0 - decay_one) * grad
    v_next = decay_two * v_ref[0] + (1.0 - decay_two) * grad * grad
    inner_next = w - inner_rate * (m_next / (jnp.sqrt(v_next) + epsilon) + weight_decay * w)
    m_out[0] = m_next
    delta_out[...] = anchor_ref[...] - inner_next


def adam(keep, recv, m, v, w, anchor):
    col = 256
    gt = pl.BlockSpec((col, SHARD), lambda j: (j, 0))
    cube = pl.BlockSpec((1, SHARD, col), lambda j: (0, 0, j))
    flat = pl.BlockSpec((SHARD, col), lambda j: (0, j))
    return pl.pallas_call(
        adam_kernel,
        grid=(KVW // col,),
        out_shape=(
            jax.ShapeDtypeStruct((1, SHARD, KVW), jnp.float32),
            jax.ShapeDtypeStruct((SHARD, KVW), jnp.float32),
        ),
        in_specs=[gt, gt, cube, cube, cube, flat],
        out_specs=(cube, flat),
        compiler_params=pltpu.CompilerParams(vmem_limit_bytes=GRANT),
        cost_estimate=pl.CostEstimate(flops=20 << 18, transcendentals=2 << 18, bytes_accessed=7 << 20),
        name="adam",
    )(keep, recv, m, v, w, anchor)


def local(acts, tok_grads, log_ratio, loss_mask, pairs, inner_w, adam_m, adam_v, anchor, outer_mom):
    f = lax.axis_index("fsdp")
    mx, mz, my = f // 8, (f // 2) % 4, f % 2
    core = lax.axis_index("rep") % 2
    bf16, f32 = jnp.bfloat16, jnp.float32

    in_hbm = lambda value: pltpu.with_memory_space_constraint(value, pltpu.HBM)
    acts = in_hbm(acts)

    def far0(k):
        return [owner(mx + k, mz + j, 0) for j in range(4)]

    def far1(k):
        return [owner(mx + j, mz + k, 1) for j in range(4)]

    tilt = (core + my) % 2

    def gathered(who, k, js):
        axis, plane = (tilt, my) if who == "own" else (1 - tilt, 1 - my)
        return [
            jnp.where(axis == 0, owner(mx + j, mz + k, plane), owner(mx + k, mz + j, plane)) for j in js
        ]

    entries = far0(2) + far1(2) + far0(1) + far0(3) + far1(1) + far1(3) + far0(0) + far1(0)
    starts = []
    every, low, high = range(4), (0, 1), (2, 3)
    for group in (
        [("own", 0, every), ("oth", 0, every), ("own", 1, high), ("own", 3, low)],
        [("own", 1, low), ("own", 3, high)],
        [("oth", 1, high), ("oth", 3, low)],
        [("oth", 1, low), ("oth", 3, high), ("own", 2, every)],
        [("oth", 2, every)],
    ):
        starts.append(len(entries))
        for entry in group:
            entries = entries + gathered(*entry)
    tab = jnp.stack(entries).astype(jnp.int32)

    where_f = f.reshape(1).astype(jnp.int32)
    row = seq_sums(where_f, in_hbm(log_ratio.reshape(ROWS // 128, 128)), in_hbm(loss_mask.reshape(ROWS // 128, 128)))
    row = row + shift(row, dy=1)
    row = row + shift(row, dx=1) + shift(row, dx=-1) + shift(row, dx=2)
    rows = (row, shift(row, dz=1), shift(row, dz=-1), shift(row, dz=2))

    w_half = inner_w[0].astype(bf16)
    one, two, three = shift_near(w_half, -1), shift_near(w_half, 2), shift_near(w_half, 1)
    row_low = jnp.concatenate([w_half, one], axis=0)
    row_high = jnp.concatenate([two, three], axis=0)
    other_low, other_high = shift(row_low, dy=1), shift(row_high, dy=1)
    next_high, prev_low = shift_far(row_high, -1), shift_far(row_low, 1)
    next_low, prev_high = shift_far(row_low, -1), shift_far(row_high, 1)
    rest = (shift(next_high, dy=1), shift(prev_low, dy=1))
    relay = (shift_far(next_low, -1), shift_far(prev_high, 1))
    cross = (shift_near(other_low, -1), shift_near(other_high, 1))
    last = (shift_near(cross[0], -1), shift_near(cross[1], 1))

    pairs_pad = jnp.pad(pairs, ((0, 0), (0, 128 - HALF)), constant_values=-1)
    cot, cott = make_cot(
        where_f, rows, pairs_pad, loss_mask.reshape(1, ROWS), loss_mask.reshape(ROWS, 1),
        tok_grads, tok_grads.T,
    )

    def big(colour, value, step):
        return shift(value, dx=step) if colour == 0 else shift(value, dz=step)

    def small(colour, value, step):
        return shift(value, dz=step) if colour == 0 else shift(value, dx=step)

    h = KVW // 2
    ups = products(split_kernel, 0, 2, h, 2, tab, cott, acts)
    terms = products(rest_kernel, 8, 6, KVW, 1, tab, cott, acts)
    sums = []
    relayed = []
    for c in (0, 1):
        relayed.append((big(c, ups[2 * c], 1), big(c, ups[2 * c + 1], -1)))
    got = []
    for c in (0, 1):
        plus = terms[2 * c].at[:h].add(relayed[c][0])
        minus = terms[2 * c + 1].at[h:].add(relayed[c][1])
        got.append((big(c, plus, 1), big(c, minus, -1)))
    for c in (0, 1):
        parts = []
        for k in range(4):
            cols = slice(k * SHARD, (k + 1) * SHARD)
            part = terms[4 + c][:, cols].astype(f32)
            part = part + got[c][0][:, cols].astype(f32) + got[c][1][:, cols].astype(f32)
            parts.append(part.astype(bf16))
        moved = [small(c, parts[k], step) for k, step in ((1, 1), (2, 2), (3, -1))]
        sums += [parts[0]] + moved
    keep, give = choose(my.reshape(1).astype(jnp.int32), sums)
    recv = in_hbm(shift(in_hbm(give), dy=1))
    new_m, delta = adam(in_hbm(keep), recv, in_hbm(adam_m), in_hbm(adam_v), in_hbm(inner_w), in_hbm(anchor))

    hs = SHARD // 2
    part = jnp.where(core == 0, delta[:hs], delta[hs:])
    other = jnp.where(core == 0, delta[hs:], delta[:hs])
    part = part + swap_rep(other, 1)
    part = part + swap_rep(part, 2)
    other = swap_rep(part, 1)
    swapped = core == 1
    total = jnp.concatenate([jnp.where(swapped, other, part), jnp.where(swapped, part, other)], axis=0)
    delta_avg = total / 4
    new_mom = momentum * outer_mom + delta_avg
    new_anchor = anchor - outer_rate * (delta_avg + momentum * new_mom)

    groups = (
        (row_low, row_high, other_low, other_high, next_high, prev_low),
        (next_low, prev_high),
        rest,
        cross + relay,
        last,
    )
    out = None
    for i, group in enumerate(groups):
        out = input_grad_part(starts[i], tab, cot, group, out)
    return (out, new_anchor, new_mom, new_m)


def solution(mesh):
    return jax.shard_map(
        local,
        mesh=mesh,
        in_specs=(
            P(("rep", "fsdp"), None),
            P(("rep", "fsdp"), None),
            P(("rep", "fsdp")),
            P(("rep", "fsdp")),
            P("rep", None),
            P("rep", "fsdp", None),
            P("rep", "fsdp", None),
            P("rep", "fsdp", None),
            P("fsdp", None),
            P("fsdp", None),
        ),
        out_specs=(
            P(("rep", "fsdp"), None),
            P("fsdp", None),
            P("fsdp", None),
            P("rep", "fsdp", None),
        ),
        check_vma=False,
    )
```

```python
import functools

import jax
import jax.numpy as jnp
from jax import lax
from jax.experimental import pallas as pl
from jax.experimental.pallas import tpu as pltpu
from jax.sharding import PartitionSpec as P


D = 8192
KVW = 1024
SEQLEN = 256
SEQ_DEV = 2
ROWS = SEQ_DEV * SEQLEN
HALF = 32
SHARD = 256

dpo_beta = 0.1
decay_one = 0.9
decay_two = 0.95
inner_rate = 0.05
weight_decay = 0.1
epsilon = 1e-08
momentum = 0.9
outer_rate = 0.7
SCALE = D ** (-0.5)


GRANT = 24 << 20


def send(value, target):
    pairs = []
    for f in range(32):
        x, z, y = target(f // 8, (f // 2) % 4, f % 2)
        pairs.append((f, (x % 4) * 8 + (z % 4) * 2 + y % 2))
    return lax.ppermute(value, "fsdp", pairs)


def shift(value, dx=0, dz=0, dy=0):
    return send(value, lambda x, z, y: (x + dx, z + dz, y + dy))


def send_tilted(value, step, far):
    pairs = []
    for i in range(128):
        rep, f = i // 32, i % 32
        x, z, y = f // 8, (f // 2) % 4, f % 2
        if (rep + y + far) % 2:
            z = (z + step) % 4
        else:
            x = (x + step) % 4
        pairs.append((i, rep * 32 + x * 8 + z * 2 + y))
    return lax.ppermute(value, ("rep", "fsdp"), pairs)


def shift_near(value, step):
    return send_tilted(value, step, 0)


def shift_far(value, step):
    return send_tilted(value, step, 1)


def swap_rep(value, bit):
    return lax.ppermute(value, "rep", [(r, r ^ bit) for r in range(4)])


def owner(x, z, y):
    return (x % 4) * 8 + (z % 4) * 2 + y


def sums_kernel(f_ref, ratio_ref, mask_ref, row_ref):
    kept = ratio_ref[...] * mask_ref[...].astype(jnp.float32)
    lane = lax.broadcasted_iota(jnp.int32, (1, 128), 1)
    row = jnp.zeros((1, 128), jnp.float32)
    rows = kept.shape[0] // SEQ_DEV
    for i in range(SEQ_DEV):
        part = jnp.sum(kept[i * rows : (i + 1) * rows], axis=0, keepdims=True)
        part = jnp.sum(part, axis=1, keepdims=True)
        row = jnp.where(lane == f_ref[0] * SEQ_DEV + i, part, row)
    row_ref[...] = row


def seq_sums(f, ratio, mask):
    vmem = pl.BlockSpec(memory_space=pltpu.VMEM)
    return pl.pallas_call(
        sums_kernel,
        out_shape=jax.ShapeDtypeStruct((1, 128), jnp.float32),
        in_specs=[pl.BlockSpec(memory_space=pltpu.SMEM), vmem, vmem],
        out_specs=vmem,
        compiler_params=pltpu.CompilerParams(vmem_limit_bytes=1 << 20),
        cost_estimate=pl.CostEstimate(flops=2048, transcendentals=0, bytes_accessed=4096),
        name="seq_sums",
    )(f, ratio, mask)


def cot_kernel(f_ref, v0_ref, v1_ref, v2_ref, v3_ref, pairs_ref, mrow_ref, mcol_ref, tg_ref, tgt_ref, cot_ref, cott_ref):
    f = f_ref[0]
    v = v0_ref[...] + v1_ref[...] + v2_ref[...] + v3_ref[...]
    row = lax.broadcasted_iota(jnp.int32, (HALF, 128), 0)
    lane = lax.broadcasted_iota(jnp.int32, (HALF, 128), 1)
    onehot = pairs_ref[...] == row
    rejected_col = jnp.sum(jnp.where(lane == row + HALF, v, 0.0), axis=1, keepdims=True)
    rejected = jnp.sum(jnp.where(onehot, rejected_col, 0.0), axis=0, keepdims=True)
    pull = jax.nn.sigmoid(-(dpo_beta * (v - rejected)))
    push = jnp.sum(jnp.where(onehot, pull, 0.0), axis=1, keepdims=True)
    lane_row = lax.broadcasted_iota(jnp.int32, (1, 128), 1)
    row_col = lax.broadcasted_iota(jnp.int32, (HALF, 1), 0)
    weights = []
    for i in range(SEQ_DEV):
        seq = f * SEQ_DEV + i
        chosen = jnp.sum(jnp.where(lane_row == seq, pull, 0.0), axis=1, keepdims=True)
        other = jnp.sum(jnp.where(row_col == seq - HALF, push, 0.0), axis=0, keepdims=True)
        weights.append(jnp.where(seq < HALF, -dpo_beta * chosen, dpo_beta * other))
    tok = lax.broadcasted_iota(jnp.int32, (1, ROWS), 1)
    wrow = jnp.where(tok < SEQLEN, weights[0], weights[1]) * mrow_ref[...].astype(jnp.float32)
    cott_ref[...] = (wrow * tgt_ref[...].astype(jnp.float32)).astype(jnp.bfloat16)
    for i in range(SEQ_DEV):
        part = slice(i * SEQLEN, (i + 1) * SEQLEN)
        wcol = weights[i] * mcol_ref[part, :].astype(jnp.float32)
        cot_ref[part, :] = (wcol * tg_ref[part, :].astype(jnp.float32)).astype(jnp.bfloat16)


def make_cot(f, rows, pairs_pad, mrow, mcol, tg, tgt):
    vmem = pl.BlockSpec(memory_space=pltpu.VMEM)
    return pl.pallas_call(
        cot_kernel,
        out_shape=(
            jax.ShapeDtypeStruct((ROWS, KVW), jnp.bfloat16),
            jax.ShapeDtypeStruct((KVW, ROWS), jnp.bfloat16),
        ),
        in_specs=[pl.BlockSpec(memory_space=pltpu.SMEM)] + [vmem] * 9,
        out_specs=(vmem, vmem),
        compiler_params=pltpu.CompilerParams(vmem_limit_bytes=GRANT),
        cost_estimate=pl.CostEstimate(flops=4_000_000, transcendentals=128, bytes_accessed=4 << 20),
        name="make_cot",
    )(f, *rows, pairs_pad, mrow, mcol, tg, tgt)


def term(cott_ref, acts_refs):
    acts = jnp.concatenate([a[...] for a in acts_refs], axis=1)
    return jnp.dot(cott_ref[...], acts, preferred_element_type=jnp.float32) * SCALE


def split_kernel(tab, cott_ref, a0, a1, *outs):
    t = term(cott_ref, (a0, a1)).astype(jnp.bfloat16)
    for colour in range(2):
        @pl.when(pl.program_id(0) // 2 == colour)
        def _(colour=colour):
            outs[2 * colour][...] = t[: KVW // 2]
            outs[2 * colour + 1][...] = t[KVW // 2 :]


def rest_kernel(tab, cott_ref, a0, a1, *outs):
    t = term(cott_ref, (a0, a1)).astype(jnp.bfloat16)
    for i, out in enumerate(outs):
        @pl.when(pl.program_id(0) // 2 == i)
        def _(out=out):
            out[...] = t


def products(kernel, first, count, rows, split, tab, cott, acts):
    spec = [
        pl.BlockSpec((rows, 2 * SHARD), lambda s, b, i=i: (0, jnp.clip(s - 2 * i, 0, 1)))
        for i in range(count)
        for _ in range(split)
    ]
    return pl.pallas_call(
        kernel,
        out_shape=(jax.ShapeDtypeStruct((rows, 4 * SHARD), jnp.bfloat16),) * (count * split),
        grid_spec=pltpu.PrefetchScalarGridSpec(
            num_scalar_prefetch=1,
            grid=(2 * count,),
            in_specs=[
                pl.BlockSpec((KVW, ROWS), lambda s, b: (0, 0)),
                pl.BlockSpec((ROWS, SHARD), lambda s, b: (0, b[first + 2 * s])),
                pl.BlockSpec((ROWS, SHARD), lambda s, b: (0, b[first + 2 * s + 1])),
            ],
            out_specs=tuple(spec),
        ),
        compiler_params=pltpu.CompilerParams(
            dimension_semantics=("arbitrary",), vmem_limit_bytes=GRANT
        ),
        cost_estimate=pl.CostEstimate(
            flops=2 * KVW * ROWS * 4 * SHARD * count, transcendentals=0, bytes_accessed=count * (3 << 20)
        ),
    )(tab, cott, acts, acts)


def input_grad_kernel(edges, tab, cot_ref, *rest):
    out_ref = rest[-1]
    for i, (low, high) in enumerate(edges):
        @pl.when((pl.program_id(0) >= low) & (pl.program_id(0) < high))
        def _(w_ref=rest[i]):
            t = lax.dot_general(
                cot_ref[...], w_ref[...], (((1,), (1,)), ((), ())), preferred_element_type=jnp.float32
            )
            out_ref[...] = (t * SCALE).astype(jnp.bfloat16)


def input_grad_part(first, tab, cot, pieces, previous):
    edges, n = [], 0
    for piece in pieces:
        edges.append((n, n + piece.shape[0] // SHARD))
        n = edges[-1][1]
    aliased = [] if previous is None else [previous]
    return pl.pallas_call(
        functools.partial(input_grad_kernel, tuple(edges)),
        out_shape=jax.ShapeDtypeStruct((ROWS, D), jnp.bfloat16),
        grid_spec=pltpu.PrefetchScalarGridSpec(
            num_scalar_prefetch=1,
            grid=(n,),
            in_specs=[pl.BlockSpec((ROWS, KVW), lambda s, b: (0, 0))]
            + [
                pl.BlockSpec((SHARD, KVW), lambda s, b, e=e: (jnp.clip(s - e[0], 0, e[1] - e[0] - 1), 0))
                for e in edges
            ]
            + [pl.BlockSpec(memory_space=pl.ANY)] * len(aliased),
            out_specs=pl.BlockSpec((ROWS, SHARD), lambda s, b: (0, b[first + s])),
        ),
        input_output_aliases={2 + len(pieces): 0} if aliased else {},
        compiler_params=pltpu.CompilerParams(
            dimension_semantics=("arbitrary",), vmem_limit_bytes=GRANT // 2
        ),
        cost_estimate=pl.CostEstimate(
            flops=2 * KVW * ROWS * n * SHARD, transcendentals=0, bytes_accessed=(1 << 20) + n * (3 << 18)
        ),
        name="input_grad",
    )(tab, cot, *pieces, *aliased)


def choose_kernel(my_ref, *refs):
    first, second = [
        sum(r[...].astype(jnp.float32) for r in refs[4 * c : 4 * c + 4]).astype(jnp.bfloat16) for c in (0, 1)
    ]
    keep_ref, give_ref = refs[8:]
    upper = my_ref[0] == 1
    keep_ref[...] = jnp.where(upper, second, first)
    give_ref[...] = jnp.where(upper, first, second)


def choose(my, parts):
    block = pl.BlockSpec((256, SHARD), lambda i: (i, 0))
    return pl.pallas_call(
        choose_kernel,
        grid=(KVW // 256,),
        out_shape=(jax.ShapeDtypeStruct((KVW, SHARD), jnp.bfloat16),) * 2,
        in_specs=[pl.BlockSpec(memory_space=pltpu.SMEM)] + [block] * 8,
        out_specs=(block, block),
        compiler_params=pltpu.CompilerParams(vmem_limit_bytes=GRANT // 3),
        cost_estimate=pl.CostEstimate(flops=2 << 20, transcendentals=0, bytes_accessed=5 << 20),
        name="choose",
    )(my, *parts)


def adam_kernel(keep_ref, recv_ref, m_ref, v_ref, w_ref, anchor_ref, m_out, delta_out):
    grad = (keep_ref[...].astype(jnp.float32) + recv_ref[...].astype(jnp.float32)).T
    w = w_ref[0]
    m_next = decay_one * m_ref[0] + (1.0 - decay_one) * grad
    v_next = decay_two * v_ref[0] + (1.0 - decay_two) * grad * grad
    inner_next = w - inner_rate * (m_next / (jnp.sqrt(v_next) + epsilon) + weight_decay * w)
    m_out[0] = m_next
    delta_out[...] = anchor_ref[...] - inner_next


def adam(keep, recv, m, v, w, anchor):
    col = 256
    gt = pl.BlockSpec((col, SHARD), lambda j: (j, 0))
    cube = pl.BlockSpec((1, SHARD, col), lambda j: (0, 0, j))
    flat = pl.BlockSpec((SHARD, col), lambda j: (0, j))
    return pl.pallas_call(
        adam_kernel,
        grid=(KVW // col,),
        out_shape=(
            jax.ShapeDtypeStruct((1, SHARD, KVW), jnp.float32),
            jax.ShapeDtypeStruct((SHARD, KVW), jnp.float32),
        ),
        in_specs=[gt, gt, cube, cube, cube, flat],
        out_specs=(cube, flat),
        compiler_params=pltpu.CompilerParams(vmem_limit_bytes=GRANT // 3),
        cost_estimate=pl.CostEstimate(flops=20 << 18, transcendentals=2 << 18, bytes_accessed=7 << 20),
        name="adam",
    )(keep, recv, m, v, w, anchor)


def local(acts, tok_grads, log_ratio, loss_mask, pairs, inner_w, adam_m, adam_v, anchor, outer_mom):
    f = lax.axis_index("fsdp")
    mx, mz, my = f // 8, (f // 2) % 4, f % 2
    core = lax.axis_index("rep") % 2
    bf16, f32 = jnp.bfloat16, jnp.float32

    in_hbm = lambda value: pltpu.with_memory_space_constraint(value, pltpu.HBM)
    acts = in_hbm(acts)

    def far0(k):
        return [owner(mx + k, mz + j, 0) for j in range(4)]

    def far1(k):
        return [owner(mx + j, mz + k, 1) for j in range(4)]

    tilt = (core + my) % 2

    def gathered(who, k, js):
        axis, plane = (tilt, my) if who == "own" else (1 - tilt, 1 - my)
        return [
            jnp.where(axis == 0, owner(mx + j, mz + k, plane), owner(mx + k, mz + j, plane)) for j in js
        ]

    entries = far0(2) + far1(2) + far0(1) + far0(3) + far1(1) + far1(3) + far0(0) + far1(0)
    starts = []
    every, low, high = range(4), (0, 1), (2, 3)
    for group in (
        [("own", 0, every), ("oth", 0, every), ("own", 1, high), ("own", 3, low)],
        [("own", 1, low), ("own", 3, high)],
        [("oth", 1, high), ("oth", 3, low)],
        [("oth", 1, low), ("oth", 3, high), ("own", 2, every)],
        [("oth", 2, every)],
    ):
        starts.append(len(entries))
        for entry in group:
            entries = entries + gathered(*entry)
    tab = jnp.stack(entries).astype(jnp.int32)

    where_f = f.reshape(1).astype(jnp.int32)
    row = seq_sums(where_f, in_hbm(log_ratio.reshape(ROWS // 128, 128)), in_hbm(loss_mask.reshape(ROWS // 128, 128)))
    row = row + shift(row, dy=1)
    row = row + shift(row, dx=1) + shift(row, dx=-1) + shift(row, dx=2)
    rows = (row, shift(row, dz=1), shift(row, dz=-1), shift(row, dz=2))

    w_half = inner_w[0].astype(bf16)
    one, two, three = shift_near(w_half, -1), shift_near(w_half, 2), shift_near(w_half, 1)
    row_low = jnp.concatenate([w_half, one], axis=0)
    row_high = jnp.concatenate([two, three], axis=0)
    other_low, other_high = shift(row_low, dy=1), shift(row_high, dy=1)
    next_high, prev_low = shift_far(row_high, -1), shift_far(row_low, 1)
    next_low, prev_high = shift_far(row_low, -1), shift_far(row_high, 1)
    rest = (shift(next_high, dy=1), shift(prev_low, dy=1))
    relay = (shift_far(next_low, -1), shift_far(prev_high, 1))
    cross = (shift_near(other_low, -1), shift_near(other_high, 1))
    last = (shift_near(cross[0], -1), shift_near(cross[1], 1))

    pairs_pad = jnp.pad(pairs, ((0, 0), (0, 128 - HALF)), constant_values=-1)
    cot, cott = make_cot(
        where_f, rows, pairs_pad, loss_mask.reshape(1, ROWS), loss_mask.reshape(ROWS, 1),
        tok_grads, tok_grads.T,
    )

    def big(colour, value, step):
        return shift(value, dx=step) if colour == 0 else shift(value, dz=step)

    def small(colour, value, step):
        return shift(value, dz=step) if colour == 0 else shift(value, dx=step)

    h = KVW // 2
    ups = products(split_kernel, 0, 2, h, 2, tab, cott, acts)
    terms = products(rest_kernel, 8, 6, KVW, 1, tab, cott, acts)
    sums = []
    relayed = []
    for c in (0, 1):
        relayed.append((big(c, ups[2 * c], 1), big(c, ups[2 * c + 1], -1)))
    got = []
    for c in (0, 1):
        plus = terms[2 * c].at[:h].add(relayed[c][0])
        minus = terms[2 * c + 1].at[h:].add(relayed[c][1])
        got.append((big(c, plus, 1), big(c, minus, -1)))
    for c in (0, 1):
        parts = []
        for k in range(4):
            cols = slice(k * SHARD, (k + 1) * SHARD)
            part = terms[4 + c][:, cols].astype(f32)
            part = part + got[c][0][:, cols].astype(f32) + got[c][1][:, cols].astype(f32)
            parts.append(part.astype(bf16))
        moved = [small(c, parts[k], step) for k, step in ((1, 1), (2, 2), (3, -1))]
        sums += [parts[0]] + moved
    keep, give = choose(my.reshape(1).astype(jnp.int32), sums)
    recv = in_hbm(shift(in_hbm(give), dy=1))
    new_m, delta = adam(in_hbm(keep), recv, in_hbm(adam_m), in_hbm(adam_v), in_hbm(inner_w), in_hbm(anchor))

    hs = SHARD // 2
    part = jnp.where(core == 0, delta[:hs], delta[hs:])
    other = jnp.where(core == 0, delta[hs:], delta[:hs])
    part = part + swap_rep(other, 1)
    part = part + swap_rep(part, 2)
    other = swap_rep(part, 1)
    total = jnp.concatenate([jnp.where(core == 0, part, other), jnp.where(core == 0, other, part)], axis=0)
    delta_avg = total / 4
    new_mom = momentum * outer_mom + delta_avg
    new_anchor = anchor - outer_rate * (delta_avg + momentum * new_mom)

    groups = (
        (row_low, row_high, other_low, other_high, next_high, prev_low),
        (next_low, prev_high),
        rest,
        cross + relay,
        last,
    )
    out = None
    for i, group in enumerate(groups):
        out = input_grad_part(starts[i], tab, cot, group, out)
    return (out, new_anchor, new_mom, new_m)


def solution(mesh):
    return jax.shard_map(
        local,
        mesh=mesh,
        in_specs=(
            P(("rep", "fsdp"), None),
            P(("rep", "fsdp"), None),
            P(("rep", "fsdp")),
            P(("rep", "fsdp")),
            P("rep", None),
            P("rep", "fsdp", None),
            P("rep", "fsdp", None),
            P("rep", "fsdp", None),
            P("fsdp", None),
            P("fsdp", None),
        ),
        out_specs=(
            P(("rep", "fsdp"), None),
            P("fsdp", None),
            P("fsdp", None),
            P("rep", "fsdp", None),
        ),
        check_vma=False,
    )
```
